128 devices in a mesh: ctx: 64 (over y_hi, z, x, core), head: 2 (over y_lo).
Axes of the slice: x: 4, y: 4 (y_hi: 2, y_lo: 2; y = y_hi * 2 + y_lo), z: 4, core: 2. Of those that a mesh axis runs over, the one named last changes fastest.
Arguments:
- queries: bfloat16 [16384, 8192], P('ctx', 'head'), may hold values from -5 to 5
- keys: bfloat16 [16384, 512], P(('ctx', 'head')), may hold values from -5 to 5
- values: bfloat16 [16384, 512], P(('ctx', 'head')), may hold values from -6 to 6
- d_out: bfloat16 [16384, 8192], P('ctx', 'head'), may hold values from -6 to 6
- selected: int32 [256, 12], P('ctx'), may hold values from 0 to 11, as said below
- partners: int32 [2, 64], replicated, may hold values from 0 to 63, as said below
Outputs:
- attended: bfloat16 [16384, 8192], P('ctx', 'head')
- grad_queries: bfloat16 [16384, 8192], P('ctx', 'head')
- grad_keys: bfloat16 [16384, 512], P(('ctx', 'head'))
- grad_values: bfloat16 [16384, 512], P(('ctx', 'head'))
The draws below stay inside these ranges and needn't reach their ends.
Inputs may be any that keep to these rules, and one draw needn't show every extreme that they name: `selected`: row b lists 12 different candidate blocks of query block b: 0 to 3 are its own shard's key blocks, 4 to 7 those of its partner under the first matching, 8 to 11 those under the second; the first entry is the query block's own key block (b modulo 4). `partners`: row r gives for every shard i its partner i XOR m_r, with a mask m_r that is the same for all shards; one of the two masks is 32, the other is 2 ** j - 1 for some j of 1 to 6, and either may stand in either row.
All inputs are finite; a program needn't handle non-finite values.
Results may differ from the reference program's by a relative error of at most 0.018.
Values may be sent and summed in bfloat16 or wider, within the bound.
No kernel may reach another device: no remote copies, remote signals or barrier semaphores. Data moves between devices by JAX's collectives and lax.ppermute only.
A program may use at most 128 MiB of HBM per device.

```python
import jax
import jax.numpy as jnp
from jax import lax

HQ = 64
KVH = 4
DH = 128
BLK = 64
SEL = 12
TOK_DEV = 256
SHARDS = 64
LOGC = 6
TOKENS = 16384
NQB = 256


def draw_queries(key, part):
    full_shape = (TOKENS, HQ * DH)
    return jnp.clip(jax.random.normal(jax.random.fold_in(key, 1), full_shape, jnp.float32), -5.0, 5.0).astype(jnp.bfloat16)


def draw_keys(key, part):
    full_shape = (TOKENS, KVH * DH)
    return jnp.clip(jax.random.normal(jax.random.fold_in(key, 2), full_shape, jnp.float32), -5.0, 5.0).astype(jnp.bfloat16)


def draw_selected(key, part):
    block_count = TOK_DEV // BLK
    cand_total = 3 * block_count
    own_block = (jnp.arange(NQB, dtype=jnp.int32) % block_count).astype(jnp.int32)
    row_keys = jax.random.split(jax.random.fold_in(key, 3), NQB)
    picked = jax.vmap(lambda row_key: jax.random.permutation(row_key, cand_total - 1)[:SEL - 1])(row_keys).astype(jnp.int32)
    others = picked + (picked >= own_block[:, None]).astype(jnp.int32)
    return jnp.concatenate([own_block[:, None], others], axis=1).astype(jnp.int32)


def draw_partners(key, part):
    half_mask = jnp.array(SHARDS // 2, jnp.int32)
    low_bits = jax.random.randint(jax.random.fold_in(key, 4), (), 1, LOGC + 1, jnp.int32)
    low_mask = (jnp.left_shift(jnp.array(1, jnp.int32), low_bits) - 1).astype(jnp.int32)
    flip = jax.random.randint(jax.random.fold_in(key, 5), (), 0, 2, jnp.int32)
    first_mask = jnp.where(flip == 1, half_mask, low_mask).astype(jnp.int32)
    second_mask = jnp.where(flip == 1, low_mask, half_mask).astype(jnp.int32)
    shard_ids = jnp.arange(SHARDS, dtype=jnp.int32)
    return jnp.stack([jnp.bitwise_xor(shard_ids, first_mask), jnp.bitwise_xor(shard_ids, second_mask)]).astype(jnp.int32)


def block_levels(own_key, shape, shards, smallest, high):
    gain = 1.0
    for axis_at, shards_of in shards:
        heights = jax.random.uniform(jax.random.fold_in(jax.random.fold_in(own_key, 6), axis_at), (shards_of,), jnp.float32, smallest / len(shards), high / len(shards))
        gain = gain * jnp.repeat(jnp.exp(heights), shape[axis_at] // shards_of).reshape((-1,) + (1,) * (len(shape) - 1 - axis_at))
    return gain


def centred(stream_key, dims, deviation, most, pieces=(), kind=jnp.bfloat16):
    loudness = block_levels(stream_key, dims, pieces, -0.22, 0.18) if pieces else 1.0
    values = jax.random.normal(stream_key, dims, jnp.float32) * deviation * loudness
    return jnp.minimum(jnp.maximum(values, -most), most).astype(kind)


def setup_inputs(seed: int = 0) -> dict:
    key_of = jax.random.split(jax.random.key(seed), 7)
    queries = draw_queries(jax.random.fold_in(key_of[6], 71), 0)
    keys = draw_keys(jax.random.fold_in(key_of[6], 71), 0)
    values = centred(key_of[2], (TOKENS, KVH * DH), 1.0, 6.0, ((0, 128),))
    d_out = centred(key_of[3], (TOKENS, HQ * DH), 1.0, 6.0, ((0, 64), (1, 2)))
    selected = draw_selected(jax.random.fold_in(key_of[6], 71), 0)
    partners = draw_partners(jax.random.fold_in(key_of[6], 71), 0)
    return dict(queries=queries, keys=keys, values=values, d_out=d_out, selected=selected, partners=partners)


def rounded(values_in):
    return lax.optimization_barrier(values_in.astype(jnp.bfloat16)).astype(jnp.float32)


def attend_shard(query_rows, cand_keys, cand_values, grad_rows, chosen_rows):
    block_count = TOK_DEV // BLK
    group_size = HQ // KVH
    score_scale = DH ** -0.5
    key_blocks = cand_keys.astype(jnp.float32).reshape(3 * block_count, BLK, KVH, DH)
    value_blocks = cand_values.astype(jnp.float32).reshape(3 * block_count, BLK, KVH, DH)
    key_terms = jnp.zeros((3 * block_count, BLK, KVH, DH), jnp.float32)
    value_terms = jnp.zeros((3 * block_count, BLK, KVH, DH), jnp.float32)
    out_parts = []
    grad_parts = []
    for block_index in range(block_count):
        row_lo = block_index * BLK
        query_block = query_rows[row_lo:row_lo + BLK].astype(jnp.float32).reshape(BLK, KVH, group_size, DH)
        grad_block = grad_rows[row_lo:row_lo + BLK].astype(jnp.float32).reshape(BLK, KVH, group_size, DH)
        chosen = chosen_rows[block_index]
        picked_keys = key_blocks[chosen].reshape(SEL * BLK, KVH, DH)
        picked_values = value_blocks[chosen].reshape(SEL * BLK, KVH, DH)
        scores = jnp.einsum("qgrd,kgd->grqk", query_block, picked_keys) * score_scale
        prob_full = jax.nn.softmax(scores, axis=-1)
        prob_low = rounded(prob_full)
        out_block = rounded(jnp.einsum("grqk,kgd->qgrd", prob_low, picked_values))
        grad_p = jnp.einsum("qgrd,kgd->grqk", grad_block, picked_values)
        row_delta = jnp.einsum("qgrd,qgrd->grq", grad_block, out_block)
        grad_s = rounded(prob_full * (grad_p - row_delta[..., None]) * score_scale)
        grad_q = rounded(jnp.einsum("grqk,kgd->qgrd", grad_s, picked_keys))
        key_part = jnp.einsum("grqk,qgrd->kgd", grad_s, query_block).reshape(SEL, BLK, KVH, DH)
        value_part = jnp.einsum("grqk,qgrd->kgd", prob_low, grad_block).reshape(SEL, BLK, KVH, DH)
        key_terms = key_terms.at[chosen].add(key_part)
        value_terms = value_terms.at[chosen].add(value_part)
        out_parts.append(out_block.reshape(BLK, HQ * DH))
        grad_parts.append(grad_q.reshape(BLK, HQ * DH))
    attended = jnp.concatenate(out_parts, 0).astype(jnp.bfloat16)
    grad_queries = jnp.concatenate(grad_parts, 0).astype(jnp.bfloat16)
    return (attended, grad_queries, key_terms.reshape(3 * TOK_DEV, KVH * DH), value_terms.reshape(3 * TOK_DEV, KVH * DH))


def reference(queries, keys, values, d_out, selected, partners):
    block_count = TOK_DEV // BLK
    query_shards = queries.reshape(SHARDS, TOK_DEV, HQ * DH)
    grad_shards = d_out.reshape(SHARDS, TOK_DEV, HQ * DH)
    key_shards = keys.reshape(SHARDS, TOK_DEV, KVH * DH)
    value_shards = values.reshape(SHARDS, TOK_DEV, KVH * DH)
    chosen_shards = selected.reshape(SHARDS, block_count, SEL)

    def one_shard(shard):
        first = partners[0, shard]
        second = partners[1, shard]
        cand_keys = jnp.concatenate([key_shards[shard], key_shards[first], key_shards[second]], 0)
        cand_values = jnp.concatenate([value_shards[shard], value_shards[first], value_shards[second]], 0)
        return attend_shard(query_shards[shard], cand_keys, cand_values, grad_shards[shard], chosen_shards[shard])

    attended, grad_queries, key_terms, value_terms = lax.map(one_shard, jnp.arange(SHARDS, dtype=jnp.int32))

    def combine(terms):
        own_part = terms[:, :TOK_DEV]
        from_first = rounded(terms[:, TOK_DEV:2 * TOK_DEV])
        from_second = rounded(terms[:, 2 * TOK_DEV:])
        total = own_part + from_first[partners[0]] + from_second[partners[1]]
        return total.astype(jnp.bfloat16).reshape(TOKENS, KVH * DH)

    return (attended.reshape(TOKENS, HQ * DH), grad_queries.reshape(TOKENS, HQ * DH), combine(key_terms), combine(value_terms))
```

```python
import functools

import jax
import jax.numpy as jnp
from jax import lax
from jax.experimental import pallas as pl
from jax.experimental.pallas import tpu as pltpu
from jax.sharding import PartitionSpec as P

KVH = 4
DH = 128
ROWS = 128
PIECES = 6
HEADS = 4
LOG2E = 1.4426950408889634
SCALE = DH ** (-0.5)
NT = (((1,), (1,)), ((), ()))
f32 = jnp.float32
bf16 = jnp.bfloat16


def attention_kernel(steps, q_ref, g_ref, *refs):
    pieces, refs = refs[:PIECES], refs[PIECES:]
    o_ref, dq_ref, refs = refs[0], refs[1], refs[2:]
    terms, refs = refs[:PIECES], refs[PIECES:]
    key_split, key_rows, val_ones, key_acc, val_acc = refs
    step = pl.program_id(0)
    group = step // steps
    tokens = q_ref.shape[0]
    count = PIECES * ROWS

    @pl.when(step == 0)
    def _():
        for g in range(2):
            for n, piece in enumerate(pieces):
                rows = slice(n * ROWS, (n + 1) * ROWS)
                k = piece[:, g * DH : (g + 1) * DH]
                v = piece[:, (2 + g) * DH : (3 + g) * DH]
                scaled = k.astype(f32) * (SCALE * LOG2E)
                high = scaled.astype(bf16)
                key_split[g, rows, :DH] = high
                key_split[g, rows, DH:] = (scaled - high.astype(f32)).astype(bf16)
                key_rows[g, rows] = k
                val_ones[g, rows, :DH] = v
                val_ones[g, rows, DH:] = jnp.ones((ROWS, DH), bf16)

    @pl.when(step % steps == 0)
    def _():
        key_acc[...] = jnp.zeros_like(key_acc)
        val_acc[...] = jnp.zeros_like(val_acc)

    cols = [slice(n * DH, (n + 1) * DH) for n in range(HEADS)]
    q = jnp.concatenate([q_ref[:, c] for c in cols], 0)
    g = jnp.concatenate([g_ref[:, c] for c in cols], 0)
    s = lax.dot_general(
        jnp.concatenate([q, q], 1), key_split[group], NT, preferred_element_type=f32
    )
    p = jnp.exp2(s - jnp.max(s, axis=1, keepdims=True))
    p_low = p.astype(bf16)
    sums = jnp.dot(p_low, val_ones[group], preferred_element_type=f32)
    inverse = 1.0 / sums[:, DH:]
    out = (sums[:, :DH] * inverse).astype(bf16)
    g_norm = g.astype(f32) * inverse
    delta = jnp.sum(g_norm * out.astype(f32), axis=1, keepdims=True)
    g_low = g_norm.astype(bf16)
    dp = lax.dot_general(g_low, val_ones[group, :, :DH], NT, preferred_element_type=f32)
    ds = (p * (dp - delta)).astype(bf16)
    dq = (jnp.dot(ds, key_rows[group], preferred_element_type=f32) * SCALE).astype(bf16)
    for n, c in enumerate(cols):
        o_ref[:, c] = out[n * tokens : (n + 1) * tokens]
        dq_ref[:, c] = dq[n * tokens : (n + 1) * tokens]
    val_acc[...] += jnp.dot(g_low.T, p_low, preferred_element_type=f32)
    key_acc[...] += jnp.dot(q.T, ds, preferred_element_type=f32)

    for g in range(2):

        @pl.when(step == (g + 1) * steps - 1)
        def _(g=g):
            for n, term in enumerate(terms):
                rows = slice(n * ROWS, (n + 1) * ROWS)
                term[:, g * DH : (g + 1) * DH] = (key_acc[:, rows] * SCALE).T.astype(term.dtype)
                term[:, (2 + g) * DH : (3 + g) * DH] = val_acc[:, rows].T.astype(term.dtype)


def attention(queries, d_out, pieces):
    tokens, width = queries.shape
    steps = width // DH // HEADS // 2
    count = PIECES * ROWS
    heads = pl.BlockSpec((tokens, DH * HEADS), lambda i: (0, i))
    whole = pl.BlockSpec((ROWS, 4 * DH), lambda i: (0, 0))
    term_types = [f32] + [bf16] * (PIECES - 1)
    results = pl.pallas_call(
        functools.partial(attention_kernel, steps),
        grid=(2 * steps,),
        in_specs=[heads, heads] + [whole] * PIECES,
        out_specs=[heads, heads] + [whole] * PIECES,
        out_shape=[jax.ShapeDtypeStruct(queries.shape, bf16)] * 2
        + [jax.ShapeDtypeStruct((ROWS, 4 * DH), t) for t in term_types],
        scratch_shapes=[
            pltpu.VMEM((2, count, 2 * DH), bf16),
            pltpu.VMEM((2, count, DH), bf16),
            pltpu.VMEM((2, count, 2 * DH), bf16),
            pltpu.VMEM((DH, count), f32),
            pltpu.VMEM((DH, count), f32),
        ],
        compiler_params=pltpu.CompilerParams(vmem_limit_bytes=48 << 20),
        cost_estimate=pl.CostEstimate(
            flops=12 * tokens * width * count,
            bytes_accessed=8 * tokens * width,
            transcendentals=tokens * width // DH * count,
        ),
        name="attention",
    )(queries, d_out, *pieces)
    return results[0], results[1], results[2:]


def exchange(value, mask, flip):
    shards, heads = lax.axis_size("ctx"), lax.axis_size("head")
    pairs = [
        (c * heads + h, (c ^ mask) * heads + (h ^ flip)) for c in range(shards) for h in range(heads)
    ]
    return lax.ppermute(value, ("ctx", "head"), pairs)


def with_masks(half, mask, queries, d_out, mine, other):
    routes = ((0, 1), (half, 0), (half, 1), (mask, 0), (mask, 1))
    arrived = [exchange(other if flip else mine, m, flip) for m, flip in routes]
    attended, grad_queries, terms = attention(queries, d_out, [mine, *arrived])
    back = [exchange(term, m, flip) for term, (m, flip) in zip(terms[1:], routes)]
    same = terms[0] + back[1].astype(f32) + back[3].astype(f32)
    cross = back[0].astype(f32) + back[2].astype(f32) + back[4].astype(f32)
    return attended, grad_queries, same.astype(bf16), cross.astype(bf16)


def body(queries, keys, values, d_out, selected, partners):
    half = lax.axis_size("ctx") // 2
    bits = lax.axis_size("ctx").bit_length() - 1
    h = lax.axis_index("head")
    width = keys.shape[1] // 2

    def columns(of):
        return jnp.concatenate(
            [lax.dynamic_slice_in_dim(x, of * width, width, 1) for x in (keys, values)], 1
        )

    mine, other = columns(h), columns(1 - h)
    low_mask = jnp.where(partners[0, 0] == half, partners[1, 0], partners[0, 0])
    which = sum((low_mask > 2**j - 1).astype(jnp.int32) for j in range(1, bits))
    attended, grad_queries, same, cross = lax.switch(
        which,
        [functools.partial(with_masks, half, 2**j - 1) for j in range(1, bits + 1)],
        queries,
        d_out,
        mine,
        other,
    )
    low = jnp.where(h == 0, same, cross)
    high = jnp.where(h == 0, cross, same)
    grad_keys = jnp.concatenate([low[:, :width], high[:, :width]], 1)
    grad_values = jnp.concatenate([low[:, width:], high[:, width:]], 1)
    return (attended, grad_queries, grad_keys, grad_values)


def solution(mesh):
    return jax.shard_map(
        body,
        mesh=mesh,
        in_specs=(
            P("ctx", "head"),
            P(("ctx", "head"), None),
            P(("ctx", "head"), None),
            P("ctx", "head"),
            P("ctx", None),
            P(),
        ),
        out_specs=(
            P("ctx", "head"),
            P("ctx", "head"),
            P(("ctx", "head"), None),
            P(("ctx", "head"), None),
        ),
        check_vma=False,
    )
```

```python
import functools

import jax
import jax.numpy as jnp
from jax import lax
from jax.experimental import pallas as pl
from jax.experimental.pallas import tpu as pltpu
from jax.sharding import PartitionSpec as P

KVH = 4
DH = 128
ROWS = 128
PIECES = 6
HEADS = 8
LOG2E = 1.4426950408889634
SCALE = DH ** (-0.5)
NT = (((1,), (1,)), ((), ()))
f32 = jnp.float32
bf16 = jnp.bfloat16


def attention_kernel(steps, q_ref, g_ref, *refs):
    pieces, refs = refs[:PIECES], refs[PIECES:]
    o_ref, dq_ref, refs = refs[0], refs[1], refs[2:]
    terms, refs = refs[:PIECES], refs[PIECES:]
    key_split, key_rows, val_ones, key_acc, val_acc = refs
    step = pl.program_id(0)
    group = step // steps
    tokens = q_ref.shape[0]
    count = PIECES * ROWS

    @pl.when(step == 0)
    def _():
        for g in range(2):
            for n, piece in enumerate(pieces):
                rows = slice(n * ROWS, (n + 1) * ROWS)
                k = piece[:, g * DH : (g + 1) * DH]
                v = piece[:, (2 + g) * DH : (3 + g) * DH]
                scaled = k.astype(f32) * (SCALE * LOG2E)
                high = scaled.astype(bf16)
                key_split[g, rows, :DH] = high
                key_split[g, rows, DH:] = (scaled - high.astype(f32)).astype(bf16)
                key_rows[g, rows] = k
                val_ones[g, rows, :DH] = v
                val_ones[g, rows, DH:] = jnp.ones((ROWS, DH), bf16)

    @pl.when(step % steps == 0)
    def _():
        key_acc[...] = jnp.zeros_like(key_acc)
        val_acc[...] = jnp.zeros_like(val_acc)

    cols = [slice(n * DH, (n + 1) * DH) for n in range(HEADS)]
    q = jnp.concatenate([q_ref[:, c] for c in cols], 0)
    g = jnp.concatenate([g_ref[:, c] for c in cols], 0)
    s = lax.dot_general(
        jnp.concatenate([q, q], 1), key_split[group], NT, preferred_element_type=f32
    )
    p = jnp.exp2(s - jnp.max(s, axis=1, keepdims=True))
    p_low = p.astype(bf16)
    sums = jnp.dot(p_low, val_ones[group], preferred_element_type=f32)
    inverse = 1.0 / sums[:, DH:]
    out = (sums[:, :DH] * inverse).astype(bf16)
    g_norm = g.astype(f32) * inverse
    delta = jnp.sum(g_norm * out.astype(f32), axis=1, keepdims=True)
    g_low = g_norm.astype(bf16)
    dp = lax.dot_general(g_low, val_ones[group, :, :DH], NT, preferred_element_type=f32)
    ds = (p * (dp - delta)).astype(bf16)
    dq = (jnp.dot(ds, key_rows[group], preferred_element_type=f32) * SCALE).astype(bf16)
    for n, c in enumerate(cols):
        o_ref[:, c] = out[n * tokens : (n + 1) * tokens]
        dq_ref[:, c] = dq[n * tokens : (n + 1) * tokens]
    val_acc[...] += jnp.dot(g_low.T, p_low, preferred_element_type=f32)
    key_acc[...] += jnp.dot(q.T, ds, preferred_element_type=f32)

    for g in range(2):

        @pl.when(step == (g + 1) * steps - 1)
        def _(g=g):
            for n, term in enumerate(terms):
                rows = slice(n * ROWS, (n + 1) * ROWS)
                term[:, g * DH : (g + 1) * DH] = (key_acc[:, rows] * SCALE).T.astype(term.dtype)
                term[:, (2 + g) * DH : (3 + g) * DH] = val_acc[:, rows].T.astype(term.dtype)


def attention(queries, d_out, pieces):
    tokens, width = queries.shape
    steps = width // DH // HEADS // 2
    count = PIECES * ROWS
    heads = pl.BlockSpec((tokens, DH * HEADS), lambda i: (0, i))
    whole = pl.BlockSpec((ROWS, 4 * DH), lambda i: (0, 0))
    term_types = [f32] + [bf16] * (PIECES - 1)
    results = pl.pallas_call(
        functools.partial(attention_kernel, steps),
        grid=(2 * steps,),
        in_specs=[heads, heads] + [whole] * PIECES,
        out_specs=[heads, heads] + [whole] * PIECES,
        out_shape=[jax.ShapeDtypeStruct(queries.shape, bf16)] * 2
        + [jax.ShapeDtypeStruct((ROWS, 4 * DH), t) for t in term_types],
        scratch_shapes=[
            pltpu.VMEM((2, count, 2 * DH), bf16),
            pltpu.VMEM((2, count, DH), bf16),
            pltpu.VMEM((2, count, 2 * DH), bf16),
            pltpu.VMEM((DH, count), f32),
            pltpu.VMEM((DH, count), f32),
        ],
        compiler_params=pltpu.CompilerParams(vmem_limit_bytes=24 << 20),
        cost_estimate=pl.CostEstimate(
            flops=12 * tokens * width * count,
            bytes_accessed=8 * tokens * width,
            transcendentals=tokens * width // DH * count,
        ),
        name="attention",
    )(*(pltpu.with_memory_space_constraint(x, pltpu.HBM) for x in (queries, d_out)), *pieces)
    return results[0], results[1], results[2:]


def exchange(value, mask, flip):
    shards, heads = lax.axis_size("ctx"), lax.axis_size("head")
    pairs = [
        (c * heads + h, (c ^ mask) * heads + (h ^ flip)) for c in range(shards) for h in range(heads)
    ]
    return lax.ppermute(value, ("ctx", "head"), pairs)


def second_mask_exchange(bits, which, first, second):
    def both(mask, x, y):
        return exchange(x, mask, 0), exchange(y, mask, 1)

    return lax.switch(
        which,
        [functools.partial(both, 2**j - 1) for j in range(1, bits + 1)],
        first,
        second,
    )


def body(queries, keys, values, d_out, selected, partners):
    half = lax.axis_size("ctx") // 2
    bits = lax.axis_size("ctx").bit_length() - 1
    h = lax.axis_index("head")
    width = keys.shape[1] // 2

    def columns(of):
        return jnp.concatenate(
            [lax.dynamic_slice_in_dim(x, of * width, width, 1) for x in (keys, values)], 1
        )

    mine, other = columns(h), columns(1 - h)
    masks = partners[:, :1]
    smaller = jnp.array([[2**j - 1 for j in range(1, bits)]], jnp.int32)
    which = jnp.sum(jnp.where((masks != half) & (masks > smaller), 1, 0))

    arrived = [exchange(other, 0, 1), exchange(mine, half, 0), exchange(other, half, 1)]
    arrived += second_mask_exchange(bits, which, mine, other)
    attended, grad_queries, terms = attention(queries, d_out, [mine, *arrived])
    back = [exchange(terms[1], 0, 1), exchange(terms[2], half, 0), exchange(terms[3], half, 1)]
    back += second_mask_exchange(bits, which, terms[4], terms[5])
    same = (terms[0] + back[1].astype(f32) + back[3].astype(f32)).astype(bf16)
    cross = (back[0].astype(f32) + back[2].astype(f32) + back[4].astype(f32)).astype(bf16)
    low = jnp.where(h == 0, same, cross)
    high = jnp.where(h == 0, cross, same)
    grad_keys = jnp.concatenate([low[:, :width], high[:, :width]], 1)
    grad_values = jnp.concatenate([low[:, width:], high[:, width:]], 1)
    return (attended, grad_queries, grad_keys, grad_values)


def solution(mesh):
    return jax.shard_map(
        body,
        mesh=mesh,
        in_specs=(
            P("ctx", "head"),
            P(("ctx", "head"), None),
            P(("ctx", "head"), None),
            P("ctx", "head"),
            P("ctx", None),
            P(),
        ),
        out_specs=(
            P("ctx", "head"),
            P("ctx", "head"),
            P(("ctx", "head"), None),
            P(("ctx", "head"), None),
        ),
        check_vma=False,
    )
```

```python
import functools

import jax
import jax.numpy as jnp
from jax import lax
from jax.experimental import pallas as pl
from jax.experimental.pallas import tpu as pltpu
from jax.sharding import PartitionSpec as P

KVH = 4
DH = 128
ROWS = 128
PIECES = 6
HEADS = 8
LOG2E = 1.4426950408889634
SCALE = DH ** (-0.5)
NT = (((1,), (1,)), ((), ()))
f32 = jnp.float32
bf16 = jnp.bfloat16


def attention_kernel(steps, q_ref, g_ref, *refs):
    pieces, refs = refs[:4], refs[4:]
    o_ref, dq_ref, refs = refs[0], refs[1], refs[2:]
    terms, refs = refs[:PIECES], refs[PIECES:]
    key_split, key_rows, val_ones, key_acc, val_acc = refs
    step = pl.program_id(0)
    group = step // steps
    tokens = q_ref.shape[0]
    count = PIECES * ROWS

    @pl.when(step == 0)
    def _():
        for g in range(2):
            end = 0
            for piece in pieces:
                rows = slice(end, end + piece.shape[0])
                end = rows.stop
                k = piece[:, g * DH : (g + 1) * DH]
                v = piece[:, (2 + g) * DH : (3 + g) * DH]
                scaled = k.astype(f32) * (SCALE * LOG2E)
                high = scaled.astype(bf16)
                key_split[g, rows, :DH] = high
                key_split[g, rows, DH:] = (scaled - high.astype(f32)).astype(bf16)
                key_rows[g, rows] = k
                val_ones[g, rows, :DH] = v
                val_ones[g, rows, DH:] = jnp.ones(k.shape, bf16)

    @pl.when(step % steps == 0)
    def _():
        key_acc[...] = jnp.zeros_like(key_acc)
        val_acc[...] = jnp.zeros_like(val_acc)

    cols = [slice(n * DH, (n + 1) * DH) for n in range(HEADS)]
    q = jnp.concatenate([q_ref[:, c] for c in cols], 0)
    g = jnp.concatenate([g_ref[:, c] for c in cols], 0)
    s = lax.dot_general(
        jnp.concatenate([q, q], 1), key_split[group], NT, preferred_element_type=f32
    )
    p = jnp.exp2(s - jnp.max(s, axis=1, keepdims=True))
    p_low = p.astype(bf16)
    sums = jnp.dot(p_low, val_ones[group], preferred_element_type=f32)
    inverse = 1.0 / sums[:, DH:]
    out = (sums[:, :DH] * inverse).astype(bf16)
    g_norm = g.astype(f32) * inverse
    delta = jnp.sum(g_norm * out.astype(f32), axis=1, keepdims=True)
    g_low = g_norm.astype(bf16)
    dp = lax.dot_general(g_low, val_ones[group, :, :DH], NT, preferred_element_type=f32)
    ds = (p * (dp - delta)).astype(bf16)
    dq = (jnp.dot(ds, key_rows[group], preferred_element_type=f32) * SCALE).astype(bf16)
    for n, c in enumerate(cols):
        o_ref[:, c] = out[n * tokens : (n + 1) * tokens]
        dq_ref[:, c] = dq[n * tokens : (n + 1) * tokens]
    val_acc[...] += jnp.dot(g_low.T, p_low, preferred_element_type=f32)
    key_acc[...] += jnp.dot(q.T, ds, preferred_element_type=f32)

    for g in range(2):

        @pl.when(step == (g + 1) * steps - 1)
        def _(g=g):
            for n, term in enumerate(terms):
                rows = slice(n * ROWS, (n + 1) * ROWS)
                term[:, g * DH : (g + 1) * DH] = (key_acc[:, rows] * SCALE).T.astype(term.dtype)
                term[:, (2 + g) * DH : (3 + g) * DH] = val_acc[:, rows].T.astype(term.dtype)


def attention(queries, d_out, pieces):
    tokens, width = queries.shape
    steps = width // DH // HEADS // 2
    count = PIECES * ROWS
    heads = pl.BlockSpec((tokens, DH * HEADS), lambda i: (0, i))
    whole = pl.BlockSpec((ROWS, 4 * DH), lambda i: (0, 0))
    term_types = [f32] + [bf16] * (PIECES - 1)
    results = pl.pallas_call(
        functools.partial(attention_kernel, steps),
        grid=(2 * steps,),
        in_specs=[heads, heads]
        + [pl.BlockSpec(x.shape, lambda i: (0, 0), pipeline_mode=pl.Buffered(1)) for x in pieces],
        out_specs=[heads, heads] + [whole] * PIECES,
        out_shape=[jax.ShapeDtypeStruct(queries.shape, bf16)] * 2
        + [jax.ShapeDtypeStruct((ROWS, 4 * DH), t) for t in term_types],
        scratch_shapes=[
            pltpu.VMEM((2, count, 2 * DH), bf16),
            pltpu.VMEM((2, count, DH), bf16),
            pltpu.VMEM((2, count, 2 * DH), bf16),
            pltpu.VMEM((DH, count), f32),
            pltpu.VMEM((DH, count), f32),
        ],
        compiler_params=pltpu.CompilerParams(vmem_limit_bytes=24 << 20),
        cost_estimate=pl.CostEstimate(
            flops=12 * tokens * width * count,
            bytes_accessed=8 * tokens * width,
            transcendentals=tokens * width // DH * count,
        ),
        name="attention",
    )(in_hbm(queries), in_hbm(d_out), *pieces)
    return results[0], results[1], results[2:]


def exchange(value, mask, flip):
    shards, heads = lax.axis_size("ctx"), lax.axis_size("head")
    pairs = [
        (c * heads + h, (c ^ mask) * heads + (h ^ flip)) for c in range(shards) for h in range(heads)
    ]
    return lax.ppermute(value, ("ctx", "head"), pairs)


def prepare_kernel(half, bits, masks_ref, k_ref, v_ref, mine_ref, other_ref, which_ref, sems):
    width = k_ref.shape[1] // 2
    h = lax.axis_index("head")
    copies = []
    for ref, of in ((other_ref, 1 - h), (mine_ref, h)):
        cols = pl.ds(pl.multiple_of(of * width, width), width)
        for part, source in enumerate((k_ref, v_ref)):
            target = ref.at[:, part * width : (part + 1) * width]
            copies.append(pltpu.make_async_copy(source.at[:, cols], target, sems.at[len(copies)]))
    for copy in copies:
        copy.start()
    first, second = masks_ref[0, 0], masks_ref[1, 0]
    low = jnp.where(first == half, second, first)
    which = jnp.int32(0)
    for j in range(1, bits):
        which += jnp.where(low > 2**j - 1, 1, 0).astype(jnp.int32)
    which_ref[0] = which
    for copy in copies:
        copy.wait()


def in_hbm(x):
    return pltpu.with_memory_space_constraint(x, pltpu.HBM)


def prepare(partners, keys, values, half, bits):
    rows, width = keys.shape
    vmem = pl.BlockSpec(memory_space=pltpu.VMEM)
    smem = pl.BlockSpec(memory_space=pltpu.SMEM)
    hbm = pl.BlockSpec(memory_space=pltpu.HBM)
    piece = jax.ShapeDtypeStruct((rows, width), bf16)
    return pl.pallas_call(
        functools.partial(prepare_kernel, half, bits),
        in_specs=[smem, hbm, hbm],
        out_specs=[vmem, vmem, smem],
        out_shape=[piece, piece, jax.ShapeDtypeStruct((1,), jnp.int32)],
        scratch_shapes=[pltpu.SemaphoreType.DMA((4,))],
        compiler_params=pltpu.CompilerParams(vmem_limit_bytes=4 << 20),
        name="prepare",
    )(*(in_hbm(x) for x in (partners, keys, values)))


def finish_kernel(own_ref, *refs):
    near, far, gk_ref, gv_ref = refs[:2], refs[2:5], refs[5], refs[6]
    width = gk_ref.shape[1] // 2
    h = lax.axis_index("head")
    same = own_ref[...] + (near[0][...].astype(f32) + near[1][...].astype(f32))
    cross = far[0][...].astype(f32) + far[1][...].astype(f32) + far[2][...].astype(f32)
    for value, of in ((same.astype(bf16), h), (cross.astype(bf16), 1 - h)):
        cols = pl.ds(pl.multiple_of(of * width, width), width)
        gk_ref[:, cols] = value[:, :width]
        gv_ref[:, cols] = value[:, width:]


def finish(own, near, far):
    vmem = pl.BlockSpec(memory_space=pltpu.VMEM)
    out = jax.ShapeDtypeStruct(own.shape, bf16)
    return pl.pallas_call(
        finish_kernel,
        in_specs=[vmem] * 6,
        out_specs=[vmem] * 2,
        out_shape=[out, out],
        compiler_params=pltpu.CompilerParams(vmem_limit_bytes=4 << 20),
        name="finish",
    )(own, *near, *far)


def by_second_mask(bits, which, branch, *operands):
    branches = [functools.partial(branch, 2**j - 1) for j in range(1, bits + 1)]
    return lax.switch(which, branches, *operands)


def body(queries, keys, values, d_out, selected, partners):
    half = lax.axis_size("ctx") // 2
    bits = lax.axis_size("ctx").bit_length() - 1
    mine, other, which = prepare(partners, keys, values, half, bits)
    which = which.reshape(())
    theirs = exchange(other, 0, 1)
    near, far = exchange(mine, half, 0), exchange(other, half, 1)
    own = jnp.concatenate([mine, theirs], 0)
    second = by_second_mask(bits, which, lambda mask, x: exchange(x, mask, 0), own)
    pieces = [own, near, far, second]
    attended, grad_queries, terms = attention(queries, d_out, pieces)
    back_theirs = exchange(terms[1], 0, 1)
    back_near, back_far = exchange(terms[2], half, 0), exchange(terms[3], half, 1)

    def back(mask, x, y):
        return exchange(x, mask, 0), exchange(y, mask, 1)

    near_second, far_second = by_second_mask(bits, which, back, terms[4], terms[5])
    grad_keys, grad_values = finish(
        terms[0], (back_near, near_second), (back_theirs, back_far, far_second)
    )
    return (attended, grad_queries, grad_keys, grad_values)


def solution(mesh):
    return jax.shard_map(
        body,
        mesh=mesh,
        in_specs=(
            P("ctx", "head"),
            P(("ctx", "head"), None),
            P(("ctx", "head"), None),
            P("ctx", "head"),
            P("ctx", None),
            P(),
        ),
        out_specs=(
            P("ctx", "head"),
            P("ctx", "head"),
            P(("ctx", "head"), None),
            P(("ctx", "head"), None),
        ),
        check_vma=False,
    )
```

```python
import functools

import jax
import jax.numpy as jnp
from jax import lax
from jax.experimental import pallas as pl
from jax.experimental.pallas import tpu as pltpu
from jax.sharding import PartitionSpec as P

KVH = 4
DH = 128
ROWS = 128
PIECES = 6
HEADS = 8
QUERY_HEADS = 4
MAIN_VMEM = 40 << 20
QUERY_VMEM = 12 << 20
LOG2E = 1.4426950408889634
SCALE = DH ** (-0.5)
NT = (((1,), (1,)), ((), ()))
f32 = jnp.float32
bf16 = jnp.bfloat16


def stack(ref, heads):
    return jnp.concatenate([ref[:, n * DH : (n + 1) * DH] for n in range(heads)], 0)


def unstack(ref, value):
    tokens = ref.shape[0]
    for n in range(ref.shape[1] // DH):
        ref[:, n * DH : (n + 1) * DH] = value[n * tokens : (n + 1) * tokens]


def fill(pieces, keys=None, split=None, vals=None, ones=None):
    end = 0
    for piece in pieces:
        rows = slice(end, end + piece.shape[0])
        end = rows.stop
        for g in range(2):
            k = piece[:, g * DH : (g + 1) * DH]
            v = piece[:, (2 + g) * DH : (3 + g) * DH]
            if keys is not None:
                keys[g, rows] = k
            if split is not None:
                scaled = k.astype(f32) * (SCALE * LOG2E)
                high = scaled.astype(bf16)
                split[g, rows, :DH] = high
                split[g, rows, DH:] = (scaled - high.astype(f32)).astype(bf16)
            if vals is not None:
                vals[g, rows] = v
            if ones is not None:
                ones[g, rows, :DH] = v
                ones[g, rows, DH:] = jnp.ones(k.shape, bf16)


def main_kernel(heads, q_hbm, g_hbm, *refs):
    pieces, refs = refs[:5], refs[5:]
    o_hbm, ds_ref, refs = refs[0], refs[1], refs[2:]
    terms, refs = refs[:PIECES], refs[PIECES:]
    q_ref, g_ref, o_ref, split, ones, key_acc, val_acc, q_sem, g_sem, o_sem = refs
    steps, tokens, width = q_ref.shape
    rows = tokens * heads

    def columns(step):
        return pl.ds(pl.multiple_of(step * width, width), width)

    def q_move(step):
        return pltpu.make_async_copy(q_hbm.at[:, columns(step)], q_ref.at[step], q_sem.at[step])

    def g_move(step):
        return pltpu.make_async_copy(g_hbm.at[:, columns(step)], g_ref.at[step], g_sem.at[step])

    def o_move(step):
        return pltpu.make_async_copy(o_ref.at[step], o_hbm.at[:, columns(step)], o_sem.at[step])

    for step in range(steps):
        q_move(step).start()
        g_move(step).start()
    fill(pieces, split=split, ones=ones)
    key_acc[...] = jnp.zeros_like(key_acc)
    val_acc[...] = jnp.zeros_like(val_acc)

    def work(step, _):
        group = step // (steps // 2)
        q_move(step).wait()
        g_move(step).wait()
        q = stack(q_ref.at[step], heads)
        g = stack(g_ref.at[step], heads)
        s = lax.dot_general(
            jnp.concatenate([q, q], 1), split[group], NT, preferred_element_type=f32
        )
        p = jnp.exp2(s - jnp.max(s, axis=1, keepdims=True))
        p_low = p.astype(bf16)
        sums = jnp.dot(p_low, ones[group], preferred_element_type=f32)
        inverse = 1.0 / sums[:, DH:]
        out = (sums[:, :DH] * inverse).astype(bf16)
        unstack(o_ref.at[step], out)
        o_move(step).start()
        g_norm = g.astype(f32) * inverse
        delta = jnp.sum(g_norm * out.astype(f32), axis=1, keepdims=True)
        g_low = g_norm.astype(bf16)
        dp = lax.dot_general(g_low, ones[group, :, :DH], NT, preferred_element_type=f32)
        ds = (p * (dp - delta)).astype(bf16)
        ds_ref[pl.ds(pl.multiple_of(step * rows, rows), rows), :] = ds
        val_acc[group] += jnp.dot(g_low.T, p_low, preferred_element_type=f32)
        key_acc[group] += jnp.dot(q.T, ds, preferred_element_type=f32)
        return 0

    lax.fori_loop(0, steps, work, 0)
    for g in range(2):
        for n, term in enumerate(terms):
            cols = slice(n * ROWS, (n + 1) * ROWS)
            key_part = (key_acc[g, :, cols] * SCALE).T.astype(term.dtype)
            term[:, g * DH : (g + 1) * DH] = key_part
            term[:, (2 + g) * DH : (3 + g) * DH] = val_acc[g, :, cols].T.astype(term.dtype)
    for step in range(steps):
        o_move(step).wait()


def query_kernel(heads, ds_ref, *refs):
    pieces, (dq_hbm, keys, dq_ref, sem) = refs[:5], refs[5:]
    steps, tokens, width = dq_ref.shape
    rows = tokens * heads
    fill(pieces, keys=keys)

    def move(step):
        cols = pl.ds(pl.multiple_of(step * width, width), width)
        return pltpu.make_async_copy(dq_ref.at[step], dq_hbm.at[:, cols], sem.at[step])

    def work(step, _):
        ds = ds_ref[pl.ds(pl.multiple_of(step * rows, rows), rows), :]
        group = step // (steps // 2)
        dq = jnp.dot(ds, keys[group], preferred_element_type=f32) * SCALE
        unstack(dq_ref.at[step], dq.astype(bf16))
        move(step).start()
        return 0

    lax.fori_loop(0, steps, work, 0)
    for step in range(steps):
        move(step).wait()


def cost(tokens, heads, keys, products, moved):
    return pl.CostEstimate(
        flops=2 * products * tokens * heads * keys * DH,
        bytes_accessed=moved,
        transcendentals=tokens * heads * keys,
    )


def main_attention(queries, d_out, pieces):
    tokens, width = queries.shape
    heads, rows = width // DH, tokens * width // DH
    count = ROWS * PIECES
    steps = heads // HEADS
    vmem = pl.BlockSpec(memory_space=pltpu.VMEM)
    hbm = pl.BlockSpec(memory_space=pltpu.HBM)
    term_types = [f32] + [bf16] * (PIECES - 1)
    results = pl.pallas_call(
        functools.partial(main_kernel, HEADS),
        in_specs=[hbm, hbm] + [vmem] * len(pieces),
        out_specs=[hbm, vmem] + [vmem] * PIECES,
        out_shape=[
            jax.ShapeDtypeStruct(queries.shape, bf16),
            jax.ShapeDtypeStruct((rows, count), bf16),
            *(jax.ShapeDtypeStruct((ROWS, 4 * DH), t) for t in term_types),
        ],
        scratch_shapes=[pltpu.VMEM((steps, tokens, DH * HEADS), bf16)] * 3
        + [pltpu.VMEM((2, count, 2 * DH), bf16)] * 2
        + [pltpu.VMEM((2, DH, count), f32)] * 2
        + [pltpu.SemaphoreType.DMA((steps,))] * 3,
        compiler_params=pltpu.CompilerParams(vmem_limit_bytes=MAIN_VMEM),
        cost_estimate=cost(tokens, heads, count, 5, 6 * tokens * width),
        name="attention",
    )(in_hbm(queries), in_hbm(d_out), *pieces)
    return results[0], results[1], results[2:]


def query_gradient(ds, tokens, pieces):
    rows, count = ds.shape
    heads = rows // tokens
    steps = heads // QUERY_HEADS
    vmem = pl.BlockSpec(memory_space=pltpu.VMEM)
    return pl.pallas_call(
        functools.partial(query_kernel, QUERY_HEADS),
        in_specs=[vmem] * (1 + len(pieces)),
        out_specs=pl.BlockSpec(memory_space=pltpu.HBM),
        out_shape=jax.ShapeDtypeStruct((tokens, heads * DH), bf16),
        scratch_shapes=[
            pltpu.VMEM((2, count, DH), bf16),
            pltpu.VMEM((steps, tokens, DH * QUERY_HEADS), bf16),
            pltpu.SemaphoreType.DMA((steps,)),
        ],
        compiler_params=pltpu.CompilerParams(vmem_limit_bytes=QUERY_VMEM),
        cost_estimate=cost(tokens, heads, count, 1, 2 * tokens * heads * DH),
        name="query_gradient",
    )(ds, *pieces)


def exchange(value, mask, flip):
    shards, heads = lax.axis_size("ctx"), lax.axis_size("head")
    pairs = [
        (c * heads + h, (c ^ mask) * heads + (h ^ flip)) for c in range(shards) for h in range(heads)
    ]
    return lax.ppermute(value, ("ctx", "head"), pairs)


def prepare_kernel(half, bits, masks_ref, k_ref, v_ref, mine_ref, other_ref, which_ref, sems):
    width = k_ref.shape[1] // 2
    h = lax.axis_index("head")
    copies = []
    for ref, of in ((other_ref, 1 - h), (mine_ref, h)):
        cols = pl.ds(pl.multiple_of(of * width, width), width)
        for part, source in enumerate((k_ref, v_ref)):
            target = ref.at[:, part * width : (part + 1) * width]
            copies.append(pltpu.make_async_copy(source.at[:, cols], target, sems.at[len(copies)]))
    for copy in copies:
        copy.start()
    first, second = masks_ref[0, 0], masks_ref[1, 0]
    low = jnp.where(first == half, second, first)
    which = jnp.int32(0)
    for j in range(1, bits):
        which += jnp.where(low > 2**j - 1, 1, 0).astype(jnp.int32)
    which_ref[0] = which
    for copy in copies:
        copy.wait()


def in_hbm(x):
    return pltpu.with_memory_space_constraint(x, pltpu.HBM)


def prepare(partners, keys, values, half, bits):
    rows, width = keys.shape
    vmem = pl.BlockSpec(memory_space=pltpu.VMEM)
    smem = pl.BlockSpec(memory_space=pltpu.SMEM)
    hbm = pl.BlockSpec(memory_space=pltpu.HBM)
    piece = jax.ShapeDtypeStruct((rows, width), bf16)
    return pl.pallas_call(
        functools.partial(prepare_kernel, half, bits),
        in_specs=[smem, hbm, hbm],
        out_specs=[vmem, vmem, smem],
        out_shape=[piece, piece, jax.ShapeDtypeStruct((1,), jnp.int32)],
        scratch_shapes=[pltpu.SemaphoreType.DMA((4,))],
        compiler_params=pltpu.CompilerParams(vmem_limit_bytes=4 << 20),
        name="prepare",
    )(*(in_hbm(x) for x in (partners, keys, values)))


def finish_kernel(own_ref, *refs):
    near, far, gk_ref, gv_ref = refs[:2], refs[2:5], refs[5], refs[6]
    width = gk_ref.shape[1] // 2
    h = lax.axis_index("head")
    same = own_ref[...] + (near[0][...].astype(f32) + near[1][...].astype(f32))
    cross = far[0][...].astype(f32) + far[1][...].astype(f32) + far[2][...].astype(f32)
    for value, of in ((same.astype(bf16), h), (cross.astype(bf16), 1 - h)):
        cols = pl.ds(pl.multiple_of(of * width, width), width)
        gk_ref[:, cols] = value[:, :width]
        gv_ref[:, cols] = value[:, width:]


def finish(own, near, far):
    vmem = pl.BlockSpec(memory_space=pltpu.VMEM)
    out = jax.ShapeDtypeStruct(own.shape, bf16)
    return pl.pallas_call(
        finish_kernel,
        in_specs=[vmem] * 6,
        out_specs=[vmem] * 2,
        out_shape=[out, out],
        compiler_params=pltpu.CompilerParams(vmem_limit_bytes=4 << 20),
        name="finish",
    )(own, *near, *far)


def by_second_mask(bits, which, branch, *operands):
    branches = [functools.partial(branch, 2**j - 1) for j in range(1, bits + 1)]
    return lax.switch(which, branches, *operands)


def body(queries, keys, values, d_out, selected, partners):
    half = lax.axis_size("ctx") // 2
    bits = lax.axis_size("ctx").bit_length() - 1
    mine, other, which = prepare(partners, keys, values, half, bits)
    which = which.reshape(())
    theirs = exchange(other, 0, 1)
    far, near = exchange(other, half, 1), exchange(mine, half, 0)
    own = jnp.concatenate([mine, theirs], 0)
    second = by_second_mask(bits, which, lambda mask, x: exchange(x, mask, 0), own)
    pieces = (mine, theirs, near, far, second)
    attended, ds, terms = main_attention(queries, d_out, pieces)
    back_theirs = exchange(terms[1], 0, 1)
    back_near, back_far = exchange(terms[2], half, 0), exchange(terms[3], half, 1)

    def back(mask, x, y, ds, *pieces):
        sent = exchange(x, mask, 0), exchange(y, mask, 1)
        return *sent, query_gradient(ds, queries.shape[0], pieces)

    near_second, far_second, grad_queries = by_second_mask(
        bits, which, back, terms[4], terms[5], ds, *pieces
    )
    grad_keys, grad_values = finish(
        terms[0], (back_near, near_second), (back_theirs, back_far, far_second)
    )
    return (attended, grad_queries, grad_keys, grad_values)


def solution(mesh):
    return jax.shard_map(
        body,
        mesh=mesh,
        in_specs=(
            P("ctx", "head"),
            P(("ctx", "head"), None),
            P(("ctx", "head"), None),
            P("ctx", "head"),
            P("ctx", None),
            P(),
        ),
        out_specs=(
            P("ctx", "head"),
            P("ctx", "head"),
            P(("ctx", "head"), None),
            P(("ctx", "head"), None),
        ),
        check_vma=False,
    )
```

```python
import functools

import jax
import jax.numpy as jnp
from jax import lax
from jax.experimental import pallas as pl
from jax.experimental.pallas import tpu as pltpu
from jax.sharding import PartitionSpec as P

KVH = 4
DH = 128
ROWS = 128
PIECES = 6
HEADS = 8
QUERY_HEADS = 4
MAIN_VMEM = 40 << 20
QUERY_VMEM = 12 << 20
LOG2E = 1.4426950408889634
SCALE = DH ** (-0.5)
NT = (((1,), (1,)), ((), ()))
f32 = jnp.float32
bf16 = jnp.bfloat16


def stack(ref, heads):
    return jnp.concatenate([ref[:, n * DH : (n + 1) * DH] for n in range(heads)], 0)


def unstack(ref, value):
    tokens = ref.shape[0]
    for n in range(ref.shape[1] // DH):
        ref[:, n * DH : (n + 1) * DH] = value[n * tokens : (n + 1) * tokens]


def fill(pieces, keys=None, split=None, vals=None, ones=None):
    end = 0
    for piece in pieces:
        rows = slice(end, end + piece.shape[0])
        end = rows.stop
        for g in range(2):
            k = piece[:, g * DH : (g + 1) * DH]
            v = piece[:, (2 + g) * DH : (3 + g) * DH]
            if keys is not None:
                keys[g, rows] = k
            if split is not None:
                scaled = k.astype(f32) * (SCALE * LOG2E)
                high = scaled.astype(bf16)
                split[g, rows, :DH] = high
                split[g, rows, DH:] = (scaled - high.astype(f32)).astype(bf16)
            if vals is not None:
                vals[g, rows] = v
            if ones is not None:
                ones[g, rows, :DH] = v
                ones[g, rows, DH:] = jnp.ones(k.shape, bf16)


def main_kernel(heads, q_hbm, g_hbm, *refs):
    pieces, refs = refs[:PIECES], refs[PIECES:]
    o_hbm, ds_ref, refs = refs[0], refs[1], refs[2:]
    terms, refs = refs[:PIECES], refs[PIECES:]
    q_ref, g_ref, o_ref, split, ones, key_acc, val_acc, q_sem, g_sem, o_sem = refs
    steps, tokens, width = q_ref.shape
    rows = tokens * heads

    def columns(step):
        return pl.ds(pl.multiple_of(step * width, width), width)

    def q_move(step):
        return pltpu.make_async_copy(q_hbm.at[:, columns(step)], q_ref.at[step], q_sem.at[step])

    def g_move(step):
        return pltpu.make_async_copy(g_hbm.at[:, columns(step)], g_ref.at[step], g_sem.at[step])

    def o_move(step):
        return pltpu.make_async_copy(o_ref.at[step], o_hbm.at[:, columns(step)], o_sem.at[step])

    for step in range(steps):
        q_move(step).start()
        g_move(step).start()
    fill(pieces, split=split, ones=ones)
    key_acc[...] = jnp.zeros_like(key_acc)
    val_acc[...] = jnp.zeros_like(val_acc)

    def work(step, _):
        group = step // (steps // 2)
        q_move(step).wait()
        g_move(step).wait()
        q = stack(q_ref.at[step], heads)
        g = stack(g_ref.at[step], heads)
        s = lax.dot_general(
            jnp.concatenate([q, q], 1), split[group], NT, preferred_element_type=f32
        )
        p = jnp.exp2(s - jnp.max(s, axis=1, keepdims=True))
        p_low = p.astype(bf16)
        sums = jnp.dot(p_low, ones[group], preferred_element_type=f32)
        inverse = 1.0 / sums[:, DH:]
        out = (sums[:, :DH] * inverse).astype(bf16)
        unstack(o_ref.at[step], out)
        o_move(step).start()
        g_norm = g.astype(f32) * inverse
        delta = jnp.sum(g_norm * out.astype(f32), axis=1, keepdims=True)
        g_low = g_norm.astype(bf16)
        dp = lax.dot_general(g_low, ones[group, :, :DH], NT, preferred_element_type=f32)
        ds = (p * (dp - delta)).astype(bf16)
        ds_ref[pl.ds(pl.multiple_of(step * rows, rows), rows), :] = ds
        val_acc[group] += jnp.dot(g_low.T, p_low, preferred_element_type=f32)
        key_acc[group] += jnp.dot(q.T, ds, preferred_element_type=f32)
        return 0

    lax.fori_loop(0, steps, work, 0)
    for g in range(2):
        for n, term in enumerate(terms):
            cols = slice(n * ROWS, (n + 1) * ROWS)
            key_part = (key_acc[g, :, cols] * SCALE).T.astype(term.dtype)
            term[:, g * DH : (g + 1) * DH] = key_part
            term[:, (2 + g) * DH : (3 + g) * DH] = val_acc[g, :, cols].T.astype(term.dtype)
    for step in range(steps):
        o_move(step).wait()


def query_kernel(heads, ds_ref, *refs):
    pieces, (dq_hbm, keys, dq_ref, sem) = refs[:PIECES], refs[PIECES:]
    steps, tokens, width = dq_ref.shape
    rows = tokens * heads
    fill(pieces, keys=keys)

    def move(step):
        cols = pl.ds(pl.multiple_of(step * width, width), width)
        return pltpu.make_async_copy(dq_ref.at[step], dq_hbm.at[:, cols], sem.at[step])

    def work(step, _):
        ds = ds_ref[pl.ds(pl.multiple_of(step * rows, rows), rows), :]
        group = step // (steps // 2)
        dq = jnp.dot(ds, keys[group], preferred_element_type=f32) * SCALE
        unstack(dq_ref.at[step], dq.astype(bf16))
        move(step).start()
        return 0

    lax.fori_loop(0, steps, work, 0)
    for step in range(steps):
        move(step).wait()


def cost(tokens, heads, keys, products, moved):
    return pl.CostEstimate(
        flops=2 * products * tokens * heads * keys * DH,
        bytes_accessed=moved,
        transcendentals=tokens * heads * keys,
    )


def main_attention(queries, d_out, pieces):
    tokens, width = queries.shape
    heads, rows = width // DH, tokens * width // DH
    count = ROWS * PIECES
    steps = heads // HEADS
    vmem = pl.BlockSpec(memory_space=pltpu.VMEM)
    hbm = pl.BlockSpec(memory_space=pltpu.HBM)
    term_types = [f32] + [bf16] * (PIECES - 1)
    results = pl.pallas_call(
        functools.partial(main_kernel, HEADS),
        in_specs=[hbm, hbm] + [vmem] * len(pieces),
        out_specs=[hbm, vmem] + [vmem] * PIECES,
        out_shape=[
            jax.ShapeDtypeStruct(queries.shape, bf16),
            jax.ShapeDtypeStruct((rows, count), bf16),
            *(jax.ShapeDtypeStruct((ROWS, 4 * DH), t) for t in term_types),
        ],
        scratch_shapes=[pltpu.VMEM((steps, tokens, DH * HEADS), bf16)] * 3
        + [pltpu.VMEM((2, count, 2 * DH), bf16)] * 2
        + [pltpu.VMEM((2, DH, count), f32)] * 2
        + [pltpu.SemaphoreType.DMA((steps,))] * 3,
        compiler_params=pltpu.CompilerParams(vmem_limit_bytes=MAIN_VMEM),
        cost_estimate=cost(tokens, heads, count, 5, 6 * tokens * width),
        name="attention",
    )(in_hbm(queries), in_hbm(d_out), *pieces)
    return results[0], results[1], results[2:]


def query_gradient(ds, tokens, pieces):
    rows, count = ds.shape
    heads = rows // tokens
    steps = heads // QUERY_HEADS
    vmem = pl.BlockSpec(memory_space=pltpu.VMEM)
    return pl.pallas_call(
        functools.partial(query_kernel, QUERY_HEADS),
        in_specs=[vmem] * (1 + len(pieces)),
        out_specs=pl.BlockSpec(memory_space=pltpu.HBM),
        out_shape=pltpu.HBM((tokens, heads * DH), bf16),
        scratch_shapes=[
            pltpu.VMEM((2, count, DH), bf16),
            pltpu.VMEM((steps, tokens, DH * QUERY_HEADS), bf16),
            pltpu.SemaphoreType.DMA((steps,)),
        ],
        compiler_params=pltpu.CompilerParams(vmem_limit_bytes=QUERY_VMEM),
        cost_estimate=cost(tokens, heads, count, 1, 2 * tokens * heads * DH),
        name="query_gradient",
    )(ds, *pieces)


def exchange(value, mask, flip):
    shards, heads = lax.axis_size("ctx"), lax.axis_size("head")
    pairs = [
        (c * heads + h, (c ^ mask) * heads + (h ^ flip)) for c in range(shards) for h in range(heads)
    ]
    return lax.ppermute(value, ("ctx", "head"), pairs)


def prepare_kernel(half, bits, masks_hbm, k_ref, v_ref, mine_ref, other_ref, which_ref, masks_ref, sems):
    width = k_ref.shape[1] // 2
    h = lax.axis_index("head")
    copies = [pltpu.make_async_copy(masks_hbm, masks_ref, sems.at[0])]
    for ref, of in ((other_ref, 1 - h), (mine_ref, h)):
        cols = pl.ds(pl.multiple_of(of * width, width), width)
        for part, source in enumerate((k_ref, v_ref)):
            target = ref.at[:, part * width : (part + 1) * width]
            copies.append(pltpu.make_async_copy(source.at[:, cols], target, sems.at[len(copies)]))
    for copy in copies:
        copy.start()
    copies[0].wait()
    first, second = masks_ref[0, 0], masks_ref[1, 0]
    low = jnp.where(first == half, second, first)
    which = jnp.int32(0)
    for j in range(1, bits):
        which += jnp.where(low > 2**j - 1, 1, 0).astype(jnp.int32)
    which_ref[0] = which
    for copy in copies[1:]:
        copy.wait()


def in_hbm(x):
    return pltpu.with_memory_space_constraint(x, pltpu.HBM)


def prepare(partners, keys, values, half, bits):
    rows, width = keys.shape
    vmem = pl.BlockSpec(memory_space=pltpu.VMEM)
    smem = pl.BlockSpec(memory_space=pltpu.SMEM)
    hbm = pl.BlockSpec(memory_space=pltpu.HBM)
    piece = jax.ShapeDtypeStruct((rows, width), bf16)
    return pl.pallas_call(
        functools.partial(prepare_kernel, half, bits),
        in_specs=[hbm, hbm, hbm],
        out_specs=[vmem, vmem, smem],
        out_shape=[piece, piece, jax.ShapeDtypeStruct((1,), jnp.int32)],
        scratch_shapes=[pltpu.SMEM(partners.shape, jnp.int32), pltpu.SemaphoreType.DMA((5,))],
        compiler_params=pltpu.CompilerParams(vmem_limit_bytes=4 << 20),
        name="prepare",
    )(*(in_hbm(x) for x in (partners, keys, values)))


def finish_kernel(own_ref, *refs):
    near, far, gk_ref, gv_ref = refs[:2], refs[2:5], refs[5], refs[6]
    width = gk_ref.shape[1] // 2
    h = lax.axis_index("head")
    same = own_ref[...] + (near[0][...].astype(f32) + near[1][...].astype(f32))
    cross = far[0][...].astype(f32) + far[1][...].astype(f32) + far[2][...].astype(f32)
    for value, of in ((same.astype(bf16), h), (cross.astype(bf16), 1 - h)):
        cols = pl.ds(pl.multiple_of(of * width, width), width)
        gk_ref[:, cols] = value[:, :width]
        gv_ref[:, cols] = value[:, width:]


def finish(own, near, far):
    vmem = pl.BlockSpec(memory_space=pltpu.VMEM)
    out = jax.ShapeDtypeStruct(own.shape, bf16)
    return pl.pallas_call(
        finish_kernel,
        in_specs=[vmem] * 6,
        out_specs=[vmem] * 2,
        out_shape=[out, out],
        compiler_params=pltpu.CompilerParams(vmem_limit_bytes=4 << 20),
        name="finish",
    )(own, *near, *far)


def by_second_mask(bits, which, branch, *operands):
    branches = [functools.partial(branch, 2**j - 1) for j in range(1, bits + 1)]
    return lax.switch(which, branches, *operands)


def body(queries, keys, values, d_out, selected, partners):
    half = lax.axis_size("ctx") // 2
    bits = lax.axis_size("ctx").bit_length() - 1
    mine, other, which = prepare(partners, keys, values, half, bits)
    which = which.reshape(())

    def gather(mask, mine, other):
        theirs = exchange(other, 0, 1)
        second_mine = exchange(mine, mask, 0)
        far, near = exchange(other, half, 1), exchange(mine, half, 0)
        return theirs, near, far, second_mine, exchange(theirs, mask, 0)

    pieces = (mine, *by_second_mask(bits, which, gather, mine, other))
    attended, ds, terms = main_attention(queries, d_out, pieces)
    back_theirs = exchange(terms[1], 0, 1)
    back_near, back_far = exchange(terms[2], half, 0), exchange(terms[3], half, 1)

    def back(mask, x, y, ds, *pieces):
        sent = exchange(x, mask, 0), exchange(y, mask, 1)
        return *sent, query_gradient(ds, queries.shape[0], pieces)

    near_second, far_second, grad_queries = by_second_mask(
        bits, which, back, terms[4], terms[5], ds, *pieces
    )
    grad_keys, grad_values = finish(
        terms[0], (back_near, near_second), (back_theirs, back_far, far_second)
    )
    return (attended, grad_queries, grad_keys, grad_values)


def solution(mesh):
    return jax.shard_map(
        body,
        mesh=mesh,
        in_specs=(
            P("ctx", "head"),
            P(("ctx", "head"), None),
            P(("ctx", "head"), None),
            P("ctx", "head"),
            P("ctx", None),
            P(),
        ),
        out_specs=(
            P("ctx", "head"),
            P("ctx", "head"),
            P(("ctx", "head"), None),
            P(("ctx", "head"), None),
        ),
        check_vma=False,
    )
```
